512 devices in a mesh: wide: 32 (over z_lo, y), narrow: 16 (over x, z_hi, core).
Axes of the slice: x: 4, y: 8, z: 8 (z_hi: 2, z_lo: 4; z = z_hi * 4 + z_lo), core: 2. Of those that a mesh axis runs over, the one named last changes fastest.
Arguments:
- features: bfloat16 [32, 16, 128, 128], P('wide', 'narrow'), may hold values from -6 to 6
- offsets: bfloat16 [32, 16, 2, 128], P('wide', 'narrow'), may hold values from 0 to 1
- counts: int32 [32, 16], P('wide', 'narrow'), may hold values from 64 to 128
- owned_pairs: int32 [32, 16, 8], P('wide', 'narrow'), may hold values from 0 to 1, as said below
- kernels: bfloat16 [8, 128, 128], replicated, may hold values from -0.1875 to 0.1875
- cotangent: bfloat16 [32, 16, 128, 128], P('wide', 'narrow'), may hold values from -6 to 6
Outputs:
- corrected: bfloat16 [32, 16, 128, 128], P('wide', 'narrow')
- grad_features: float32 [32, 16, 128, 128], P('wide', 'narrow')
- grad_kernels: float32 [8, 128, 128], replicated
The draws below stay inside these ranges and needn't reach their ends.
Inputs may be any that keep to these rules, and one draw needn't show every extreme that they name: owned_pairs[x, y, s] = 1 means that the device of cell (x, y) evaluates the pair of tower cell (x, y + a) and plate cell (x + b, y), indices modulo 32 and 16, with (a, b) the s-th of (0,1), (0,-1), (-1,0), (1,0), (-1,1), (1,-1), (1,1), (-1,-1). Each unordered pair of distinct cells whose indices differ by at most one in each dimension is evaluated at most once, by one of its two candidate devices. Some device evaluates all 8.
All inputs are finite; a program needn't handle non-finite values.
Results may differ from the reference program's by a relative error of at most 0.0075.
Values may be sent and summed in bfloat16 or wider, within the bound.
No kernel may reach another device: no remote copies, remote signals or barrier semaphores. Data moves between devices by JAX's collectives and lax.ppermute only.
A program may use at most 64 MiB of HBM per device.

```python
import math
from functools import partial
import jax
import jax.numpy as jnp
from jax import lax

C = 128
K = 8
P_SIZE = 128
NW = 32
NN = 16


def draw_owned_pairs(key, part):
    first_key, second_key, third_key, fourth_key, fifth_key = jax.random.split(key, 5)
    band_width = max(NW // 4, 1)
    band_shift = jax.random.randint(first_key, (), 0, NW)
    stripe = (jnp.arange(NW) + band_shift) // band_width % 2
    threshold = 1 + 6 * stripe
    dice_roll = jax.random.randint(second_key, (NW, NN, 4), 0, 8)
    orientation = (dice_roll >= threshold[:, None, None]).astype(jnp.int32)
    listed = jax.random.randint(third_key, (NW, NN, 4), 0, 4) > 0
    flag_table = jnp.where(listed, orientation, 2).astype(jnp.int32)
    hot_col = jax.random.randint(fourth_key, (), 0, NW)
    hot_row = jax.random.randint(fifth_key, (), 0, NN)
    left_col = (hot_col - 1) % NW
    lower_row = (hot_row - 1) % NN
    upper_row = (hot_row + 1) % NN
    flag_table = flag_table.at[hot_col, hot_row, 0].set(0)
    flag_table = flag_table.at[left_col, hot_row, 0].set(1)
    flag_table = flag_table.at[hot_col, lower_row, 1].set(0)
    flag_table = flag_table.at[hot_col, hot_row, 1].set(1)
    flag_table = flag_table.at[hot_col, lower_row, 2].set(0)
    flag_table = flag_table.at[left_col, hot_row, 2].set(1)
    flag_table = flag_table.at[hot_col, upper_row, 3].set(0)
    flag_table = flag_table.at[left_col, hot_row, 3].set(1)
    first_dir = flag_table[:, :, 0]
    second_dir = flag_table[:, :, 1]
    third_dir = flag_table[:, :, 2]
    fourth_dir = flag_table[:, :, 3]
    slot_list = [first_dir == 0, jnp.roll(first_dir, 1, axis=0) == 1, jnp.roll(second_dir, 1, axis=1) == 0, second_dir == 1, jnp.roll(third_dir, 1, axis=1) == 0, jnp.roll(third_dir, 1, axis=0) == 1, jnp.roll(fourth_dir, -1, axis=1) == 0, jnp.roll(fourth_dir, 1, axis=0) == 1]
    return jnp.stack(slot_list, axis=-1).astype(jnp.int32)


def set_ends(values, stream_key, least, high):
    index_at = [jax.random.randint(jax.random.fold_in(stream_key, axis), (), 0, length) for axis, length in enumerate(values.shape)]
    longest = values.shape.index(max(values.shape))
    beside = index_at[:longest] + [(index_at[longest] + 1) % values.shape[longest]] + index_at[longest + 1:]
    return values.at[tuple(index_at)].set(least).at[tuple(beside)].set(high)


def block_scale(own_key, dims, cuts, least, top_value):
    loudness = 1.0
    for dim, shards_of in cuts:
        draws = jax.random.uniform(jax.random.fold_in(jax.random.fold_in(own_key, 6), dim), (shards_of,), jnp.float32, least / len(cuts), top_value / len(cuts))
        loudness = loudness * jnp.repeat(jnp.exp(draws), dims[dim] // shards_of).reshape((-1,) + (1,) * (len(dims) - 1 - dim))
    return loudness


def scatter_about(key, extent, width, reach, cuts=(), held_as=jnp.bfloat16):
    gain = block_scale(key, extent, cuts, -0.22, 0.18) if cuts else 1.0
    entries = jax.random.normal(key, extent, jnp.float32) * width * gain
    return jnp.minimum(jnp.maximum(entries, -reach), reach).astype(held_as)


def setup_inputs(seed: int = 0) -> dict:
    splits = jax.random.split(jax.random.key(seed), 7)
    return {
        "features": scatter_about(splits[0], (NW, NN, P_SIZE, C), 1.0, 6.0, ((0, 32), (1, 16))),
        "offsets": jnp.clip(1.0 * jax.random.uniform(splits[1], (NW, NN, 2, P_SIZE), jnp.float32) ** block_scale(splits[1], (NW, NN, 2, P_SIZE), ((0, 32), (1, 16)), -0.2, 0.2), 0.0, 1.0).astype(jnp.bfloat16),
        "counts": set_ends(jax.random.randint(splits[2], (NW, NN), P_SIZE // 2, P_SIZE + 1), jax.random.fold_in(splits[2], 1), P_SIZE // 2, P_SIZE).astype(jnp.int32),
        "owned_pairs": draw_owned_pairs(jax.random.fold_in(splits[6], 71), 0),
        "kernels": scatter_about(splits[4], (K, C, C), (K * C) ** -0.5, 0.1875),
        "cotangent": scatter_about(splits[5], (NW, NN, P_SIZE, C), 1.0, 6.0, ((0, 32), (1, 16))),
    }


KERNEL_SCALE = 0.0625
SLOT_SHIFTS = ((0, 1), (0, -1), (-1, 0), (1, 0), (-1, 1), (1, -1), (1, 1), (-1, -1))

def round_half(values):
    return lax.optimization_barrier(values.astype(jnp.bfloat16)).astype(jnp.float32)

def kernel_terms(tower_geom, plate_geom, row_shift, col_shift):
    delta_x = plate_geom[..., 0, None, :] + col_shift - tower_geom[..., 0, :, None]
    delta_y = plate_geom[..., 1, None, :] - row_shift - tower_geom[..., 1, :, None]
    square = delta_x * delta_x + delta_y * delta_y
    radius = jnp.sqrt(square)
    window = jnp.square(jnp.maximum(1.0 - square, 0.0))
    weight = KERNEL_SCALE * window * tower_geom[..., 2, :, None] * plate_geom[..., 2, None, :]
    pieces = []
    for level_index in range(4):
        bump_term = weight * jnp.maximum(1.0 - jnp.abs(3.0 * radius - level_index), 0.0)
        pieces.append(bump_term * delta_x)
        pieces.append(bump_term * delta_y)
    return jnp.stack(pieces, axis=-3)

def column_terms(row_shift, col_shift, matrices, inputs):
    tower_geom, plate_geom, tower_h, plate_h, tower_g, plate_g, tower_proj, plate_proj, active = inputs
    kernel_f32 = kernel_terms(tower_geom, plate_geom, row_shift, col_shift) * active[:, None, None, None]
    row_sums = lax.optimization_barrier(jnp.sum(kernel_f32, axis=3))
    col_sums = lax.optimization_barrier(jnp.sum(kernel_f32, axis=2))
    kernel_half = round_half(kernel_f32)
    tower_mix = round_half(row_sums[..., None] * tower_h[:, None] + jnp.einsum('ykij,yjc->ykic', kernel_half, plate_h))
    plate_mix = round_half(jnp.einsum('ykij,yic->ykjc', kernel_half, tower_h) + col_sums[..., None] * plate_h[:, None])
    tower_force = jnp.einsum('ykic,kcd->yid', tower_mix, matrices)
    plate_force = -jnp.einsum('ykjc,kcd->yjd', plate_mix, matrices)
    tower_grad = lax.optimization_barrier(jnp.sum(row_sums[..., None] * tower_proj, axis=1)) - jnp.einsum('ykij,ykjc->yic', kernel_half, plate_proj)
    plate_grad = jnp.einsum('ykij,ykic->yjc', kernel_half, tower_proj) - lax.optimization_barrier(jnp.sum(col_sums[..., None] * plate_proj, axis=1))
    kernel_part = jnp.einsum('ykic,yid->kcd', tower_mix, tower_g) - jnp.einsum('ykjc,yjd->kcd', plate_mix, plate_g)
    return (tower_force, plate_force, tower_grad, plate_grad, kernel_part)

def reference(features, offsets, counts, owned_pairs, kernels, cotangent):
    live_mask = (jnp.arange(P_SIZE, dtype=jnp.int32)[None, None, :] < counts[:, :, None]).astype(jnp.float32)
    geometry = jnp.concatenate([offsets.astype(jnp.float32), live_mask[:, :, None, :]], axis=2)
    hidden = features.astype(jnp.float32)
    upstream = cotangent.astype(jnp.float32)
    matrices = kernels.astype(jnp.float32)
    projected = round_half(jnp.einsum('xyid,kcd->xykic', upstream, matrices))
    force_sum = jnp.zeros(hidden.shape, jnp.float32)
    grad_sum = jnp.zeros(hidden.shape, jnp.float32)
    kernel_sum = jnp.zeros(matrices.shape, jnp.float32)
    shifts = list(SLOT_SHIFTS) + [(0, 0)]
    for slot_index, (row_shift, col_shift) in enumerate(shifts):
        if slot_index < 8:
            active = owned_pairs[:, :, slot_index].astype(jnp.float32)
        else:
            active = jnp.ones(live_mask.shape[:2], jnp.float32)
        inputs = (jnp.roll(geometry, -row_shift, axis=1), jnp.roll(geometry, -col_shift, axis=0), jnp.roll(hidden, -row_shift, axis=1), jnp.roll(hidden, -col_shift, axis=0), jnp.roll(upstream, -row_shift, axis=1), jnp.roll(upstream, -col_shift, axis=0), jnp.roll(projected, -row_shift, axis=1), jnp.roll(projected, -col_shift, axis=0), active)
        tower_force, plate_force, tower_grad, plate_grad, kernel_parts = lax.map(partial(column_terms, row_shift, col_shift, matrices), inputs)
        kernel_sum = kernel_sum + lax.optimization_barrier(jnp.sum(kernel_parts, axis=0))
        force_sum = force_sum + jnp.roll(tower_force, row_shift, axis=1) + jnp.roll(plate_force, col_shift, axis=0)
        grad_sum = grad_sum + jnp.roll(tower_grad, row_shift, axis=1) + jnp.roll(plate_grad, col_shift, axis=0)
    return (force_sum.astype(jnp.bfloat16), grad_sum, kernel_sum / math.sqrt(NW * NN * P_SIZE))
```

```python
import jax
import jax.numpy as jnp
from jax import lax
from jax.experimental import pallas as pl
from jax.experimental.pallas import tpu as pltpu
from jax.sharding import Mesh, PartitionSpec as P

SLOT_SHIFTS = ((0, 1), (0, -1), (-1, 0), (1, 0), (-1, 1), (1, -1), (1, 1), (-1, -1))
SLOT = {shift: index for index, shift in enumerate(SLOT_SHIFTS)}
KERNEL_SCALE = 0.0625
FAR = 64.0
K, N, C = 8, 128, 128
GEO = 2 * N
ROWS = 2 * N + 16
LIVE, FLAG = GEO + 2, GEO + 3
WIDE = ("zl", "y")
NARROW = ("x", "zh", "core")
GROUP = ("y", "x", "core")
DEPTH = ("zl", "zh")
BF16, F32 = jnp.bfloat16, jnp.float32


def pack_kernel(counts, owned, features, cotangent, offsets, out):
    out[0:N, :] = features[...]
    out[N:GEO, :] = cotangent[...]
    row = lax.broadcasted_iota(jnp.int32, (16, N), 0)
    lane = lax.broadcasted_iota(jnp.int32, (16, N), 1)
    off = offsets[...].astype(F32)
    geo = jnp.where(row == 0, off[0:1, :], jnp.where(row == 1, off[1:2, :], 0.0))
    geo = jnp.where((row == 2) & (lane < counts[0, 0]), 1.0, geo)
    for s in range(8):
        geo = jnp.where(row == 3 + s, owned[0, s].astype(F32), geo)
    out[GEO:ROWS, :] = geo.astype(BF16)


def pack(counts, owned, features, cotangent, offsets):
    smem = pl.BlockSpec(memory_space=pltpu.SMEM)
    vmem = pl.BlockSpec(memory_space=pltpu.VMEM)
    return pl.pallas_call(
        pack_kernel,
        out_shape=jax.ShapeDtypeStruct((ROWS, C), BF16),
        in_specs=[smem, smem, vmem, vmem, vmem],
        out_specs=vmem,
        name="pack",
    )(counts, owned, features, cotangent, offsets)


def pair_kernel(middle, left, right, kernels, corrected, grad, part, s_ref, x_ref, r_ref, t_ref, z_ref, w_ref, p_ref):
    columns = {0: middle, -1: left, 1: right}
    base = {0: 0, 1: ROWS, -1: 2 * ROWS}

    def geo(dx, dy, row):
        at = base[dy] + row
        return columns[dx][at : at + 1, :].astype(F32)

    cells = [(0, 0)] + [(dx, dy) for dx in (0, -1, 1) for dy in (0, 1, -1) if dx or dy]
    for n, (dx, dy) in enumerate(cells):
        use = geo(dx, dy, LIVE)
        if dx or dy:
            use = use * (geo(0, dy, FLAG + SLOT[(-dy, dx)]) + geo(dx, 0, FLAG + SLOT[(dy, -dx)]))
        px = jnp.where(use > 0.5, geo(dx, dy, GEO) + dx, -FAR)
        py = geo(dx, dy, GEO + 1) + dy
        p_ref[2 * n : 2 * n + 1, :] = px
        p_ref[2 * n + 1 : 2 * n + 2, :] = py
        source, at = columns[dx], base[dy]
        x_ref[n * N : (n + 1) * N, 0:C] = source[at : at + N, :]
        x_ref[n * N : (n + 1) * N, C : 2 * C] = source[at + N : at + GEO, :]

    own_x = jnp.where(geo(0, 0, LIVE) > 0.5, geo(0, 0, GEO), FAR)
    own_y = geo(0, 0, GEO + 1)
    t_ref[0:N, 0:N] = jnp.broadcast_to(own_x, (N, N)).T
    t_ref[0:N, N : 2 * N] = jnp.broadcast_to(own_y, (N, N)).T

    def rows(step, carry):
        at = pl.multiple_of(step * 16, 16)
        ax = t_ref[pl.ds(at, 16), 0:N]
        ay = t_ref[pl.ds(at, 16), N : 2 * N]
        sums = [None] * K
        for n in range(len(cells)):
            u = p_ref[2 * n : 2 * n + 1, :] - ax
            v = p_ref[2 * n + 1 : 2 * n + 2, :] - ay
            square = u * u + v * v
            t = square * (3.0 * lax.rsqrt(jnp.maximum(square, 1e-30)))
            low = jnp.maximum(1.0 - square, 0.0)
            window = low * low
            if n == 0:
                window = window + window
            hats = (
                jnp.maximum(1.0 - t, 0.0),
                jnp.maximum(jnp.minimum(t, 2.0 - t), 0.0),
                jnp.maximum(jnp.minimum(t - 1.0, 3.0 - t), 0.0),
                jnp.maximum(t - 2.0, 0.0),
            )
            for q in range(4):
                weight = window * hats[q]
                for k, term in ((2 * q, weight * u), (2 * q + 1, weight * v)):
                    sums[k] = term if n == 0 else sums[k] + term
                    s_ref[pl.ds(k * N + at, 16), n * N : (n + 1) * N] = term.astype(BF16)
        for k in range(K):
            total = jnp.sum(sums[k], axis=1, keepdims=True)
            r_ref[pl.ds(k * N + at, 16), :] = jnp.broadcast_to(total, (16, N))
        return carry

    lax.fori_loop(0, N // 16, rows, 0)

    t_ref[...] = jnp.dot(s_ref[...], x_ref[...], preferred_element_type=F32)
    f = middle[0:N, :].astype(F32)
    g = middle[N:GEO, :].astype(F32)
    for k in range(K):
        r = r_ref[k * N : (k + 1) * N, :]
        z_ref[:, k * C : (k + 1) * C] = (r * f + t_ref[k * N : (k + 1) * N, 0:C]).astype(BF16)
        w_ref[:, k * C : (k + 1) * C] = (r * g - t_ref[k * N : (k + 1) * N, C : 2 * C]).astype(BF16)
    own_g = middle[N:GEO, :]
    part[...] = lax.dot_general(z_ref[...], own_g, (((0,), (0,)), ((), ())), preferred_element_type=F32).astype(BF16)
    force = jnp.dot(z_ref[...], kernels[...], preferred_element_type=F32)
    corrected[...] = (force * KERNEL_SCALE).astype(BF16)
    total = None
    for k in range(K):
        term = lax.dot_general(
            w_ref[:, k * C : (k + 1) * C],
            kernels[k * C : (k + 1) * C, :],
            (((1,), (1,)), ((), ())),
            preferred_element_type=F32,
        )
        total = term if total is None else total + term
    grad[...] = total * KERNEL_SCALE


def evaluate(middle, left, right, kernels):
    vmem = pl.BlockSpec(memory_space=pltpu.VMEM)
    return pl.pallas_call(
        pair_kernel,
        out_shape=(
            jax.ShapeDtypeStruct((N, C), BF16),
            jax.ShapeDtypeStruct((N, C), F32),
            jax.ShapeDtypeStruct((K * C, C), BF16),
        ),
        in_specs=[vmem] * 4,
        out_specs=(vmem,) * 3,
        scratch_shapes=[
            pltpu.VMEM((K * N, 9 * N), BF16),
            pltpu.VMEM((9 * N, 2 * C), BF16),
            pltpu.VMEM((K * N, N), F32),
            pltpu.VMEM((K * N, 2 * C), F32),
            pltpu.VMEM((N, K * C), BF16),
            pltpu.VMEM((N, K * C), BF16),
            pltpu.VMEM((24, N), F32),
        ],
        name="pairs",
    )(middle, left, right, kernels)


def shifted(value, axes, steps):
    count = lax.axis_size(axes)
    return lax.ppermute(value, axes, [(source, (source + steps) % count) for source in range(count)])


def exchanged(blocks, axes):
    return lax.all_to_all(blocks, axes, 0, 0, tiled=False)


def added(blocks):
    return jnp.sum(blocks.astype(F32), axis=0).astype(BF16)


def whole_sum(part):
    group, depth = lax.axis_size(GROUP), lax.axis_size(DEPTH)
    piece = added(exchanged(part.reshape(group, -1, C), GROUP))
    piece = added(exchanged(jnp.broadcast_to(piece, (depth,) + piece.shape), DEPTH))
    return exchanged(jnp.broadcast_to(piece, (group,) + piece.shape), GROUP).reshape(K, C, C)


def body(features, offsets, counts, owned_pairs, kernels, cotangent):
    own = pack(counts, owned_pairs[0], features[0, 0], cotangent[0, 0], offsets[0, 0])
    below, above = shifted(own, NARROW, 1), shifted(own, NARROW, -1)
    middle = jnp.concatenate([own, above, below])
    left, right = shifted(middle, WIDE, 1), shifted(middle, WIDE, -1)
    corrected, grad, part = evaluate(middle, left, right, kernels.reshape(K * C, C))
    scale = KERNEL_SCALE / float(lax.axis_size(WIDE) * lax.axis_size(NARROW) * N) ** 0.5
    weights = whole_sum(part).astype(F32) * scale
    return corrected[None, None], grad[None, None], weights


def solution(mesh):
    split = Mesh(mesh.devices.reshape(4, 8, 4, 2, 2), ("zl", "y", "x", "zh", "core"))
    cell = P(WIDE, NARROW)
    return jax.shard_map(
        body,
        mesh=split,
        in_specs=(cell, cell, cell, cell, P(), cell),
        out_specs=(cell, cell, P()),
        check_vma=False,
    )
```

```python
import jax
import jax.numpy as jnp
from jax import lax
from jax.experimental import pallas as pl
from jax.experimental.pallas import tpu as pltpu
from jax.sharding import Mesh, PartitionSpec as P


SLOT_SHIFTS = ((0, 1), (0, -1), (-1, 0), (1, 0), (-1, 1), (1, -1), (1, 1), (-1, -1))
SLOT = {shift: index for index, shift in enumerate(SLOT_SHIFTS)}
KERNEL_SCALE = 0.0625
FAR = 64.0
K, N, C = 8, 128, 128
GEO = 2 * N
ROWS = 2 * N + 16
HALF = K * C // 2
LIVE, FLAG, SIDES = GEO + 2, GEO + 3, GEO + 11
WIDE = ("zl", "y")
NARROW = ("x", "zh", "core")
GROUP = ("y", "x")
DEPTH = ("zl", "zh")
BF16, F32 = jnp.bfloat16, jnp.float32
HERE = pl.BlockSpec(memory_space=pltpu.VMEM)
LIMIT = pltpu.CompilerParams(vmem_limit_bytes=16 << 20)


def held(value):
    return pltpu.with_memory_space_constraint(value, pltpu.VMEM)


def pack_kernel(counts, owned_hbm, features, cotangent, offsets, out, owned, off_ref, sems):
    copies = (
        pltpu.make_async_copy(offsets, off_ref, sems.at[0]),
        pltpu.make_async_copy(features, out.at[0:N], sems.at[1]),
        pltpu.make_async_copy(cotangent, out.at[N:GEO], sems.at[2]),
        pltpu.make_async_copy(owned_hbm, owned, sems.at[3]),
    )
    for copy in copies:
        copy.start()
    row = lax.broadcasted_iota(jnp.int32, (16, N), 0)
    lane = lax.broadcasted_iota(jnp.int32, (16, N), 1)
    copies[0].wait()
    copies[3].wait()
    off = off_ref[...].astype(F32)
    geo = jnp.where(row == 0, off[0:1, :], jnp.where(row == 1, off[1:2, :], 0.0))
    geo = jnp.where((row == 2) & (lane < counts[0, 0]), 1.0, geo)
    for s in range(8):
        geo = jnp.where(row == 3 + s, owned[0, s].astype(F32), geo)
    geo = jnp.where(row == 11, 1.0 - 2.0 * (lax.axis_index("y") % 2).astype(F32), geo)
    geo = jnp.where(row == 12, 1.0 - 2.0 * lax.axis_index("core").astype(F32), geo)
    out[GEO:ROWS, :] = geo.astype(BF16)
    copies[1].wait()
    copies[2].wait()


def pack(counts, owned, features, cotangent, offsets):
    smem = pl.BlockSpec(memory_space=pltpu.SMEM)
    hbm = pl.BlockSpec(memory_space=pltpu.HBM)
    return pl.pallas_call(
        pack_kernel,
        out_shape=pltpu.VMEM((ROWS, C), BF16),
        in_specs=[smem, hbm, hbm, hbm, hbm],
        out_specs=HERE,
        scratch_shapes=[pltpu.SMEM((1, 8), jnp.int32), pltpu.VMEM((2, N), BF16), pltpu.SemaphoreType.DMA((4,))],
        compiler_params=LIMIT,
        name="pack",
    )(counts, *(pltpu.with_memory_space_constraint(value, pltpu.HBM) for value in (owned, features, cotangent, offsets)))


def stack_kernel(first, second, third, out):
    out[0:ROWS, :] = first[...]
    out[ROWS : 2 * ROWS, :] = second[...]
    out[2 * ROWS : 3 * ROWS, :] = third[...]


def stacked(first, second, third):
    return pl.pallas_call(
        stack_kernel,
        out_shape=pltpu.VMEM((3 * ROWS, C), BF16),
        in_specs=[HERE] * 3,
        out_specs=HERE,
        compiler_params=LIMIT,
        name="stack",
    )(held(first), held(second), held(third))


def build(cells, own_ref, p_ref, s_ref, store_sums, double_first):
    def rows(step, carry):
        at = pl.multiple_of(step * 16, 16)
        ax = own_ref[pl.ds(at, 16), 0:N]
        ay = own_ref[pl.ds(at, 16), N : 2 * N]
        sums = [None] * K
        for n in range(cells):
            u = p_ref[2 * n : 2 * n + 1, :] - ax
            v = p_ref[2 * n + 1 : 2 * n + 2, :] - ay
            square = u * u + v * v
            t = square * (3.0 * lax.rsqrt(jnp.maximum(square, 1e-30)))
            low = jnp.maximum(1.0 - square, 0.0)
            window = low * low
            if n == 0 and double_first:
                window = window + window
            hats = (
                jnp.maximum(1.0 - t, 0.0),
                jnp.maximum(jnp.minimum(t, 2.0 - t), 0.0),
                jnp.maximum(jnp.minimum(t - 1.0, 3.0 - t), 0.0),
                jnp.maximum(t - 2.0, 0.0),
            )
            for q in range(4):
                weight = window * hats[q]
                for k, term in ((2 * q, weight * u), (2 * q + 1, weight * v)):
                    sums[k] = term if n == 0 else sums[k] + term
                    s_ref[pl.ds(k * N + at, 16), n * N : (n + 1) * N] = term.astype(BF16)
        store_sums(at, sums)
        return carry

    lax.fori_loop(0, N // 16, rows, 0)


def line(block, row):
    return block[row : row + 1, :].astype(F32)


def flag_of(block, at, flip, towards_x, towards_y, right, above):
    def row(dx, dy):
        return line(block, at + FLAG + SLOT[(-flip * dy, flip * dx)])

    def along(dx):
        if not towards_y:
            return row(dx, 0)
        return jnp.where(above, row(dx, towards_y), row(dx, -towards_y))

    if not towards_x:
        return along(0)
    return jnp.where(right, along(towards_x), along(-towards_x))


def place(block, at, use, shift_x, shift_y, p_ref, n):
    p_ref[2 * n : 2 * n + 1, :] = jnp.where(use > 0.5, line(block, at + GEO) + shift_x, -FAR)
    p_ref[2 * n + 1 : 2 * n + 2, :] = line(block, at + GEO + 1) + shift_y


def gather(block, at, x_ref, n):
    x_ref[n * N : (n + 1) * N, 0:C] = block[at : at + N, :]
    x_ref[n * N : (n + 1) * N, C : 2 * C] = block[at + N : at + GEO, :]


def near_kernel(own, narrow0, narrow1, total, sums_out, own_out, s_ref, x_ref, p_ref):
    sy = line(own, SIDES + 1)
    above = sy > 0
    place(own, 0, line(own, LIVE), 0.0, 0.0, p_ref, 0)
    gather(own, 0, x_ref, 0)
    for n, side, block in ((1, 1, narrow0), (2, -1, narrow1)):
        active = flag_of(own, 0, -1, 0, side, None, above) + flag_of(block, 0, 1, 0, side, None, above)
        place(block, 0, line(block, LIVE) * active, 0.0, side * sy, p_ref, n)
        gather(block, 0, x_ref, n)

    own_x = jnp.where(line(own, LIVE) > 0.5, line(own, GEO), FAR)
    own_out[:, 0:N] = jnp.broadcast_to(own_x, (N, N)).T
    own_out[:, N : 2 * N] = jnp.broadcast_to(line(own, GEO + 1), (N, N)).T

    def store_sums(at, sums):
        for k in range(K):
            sums_out[pl.ds(k * N + at, 16), :] = sums[k]

    build(3, own_out, p_ref, s_ref, store_sums, True)
    total[...] = jnp.dot(s_ref[...], x_ref[...], preferred_element_type=F32)


def near(stack):
    return pl.pallas_call(
        near_kernel_stacked,
        out_shape=(
            pltpu.VMEM((K * N, 2 * C), F32),
            pltpu.VMEM((K * N, N), F32),
            pltpu.VMEM((N, 2 * N), F32),
        ),
        in_specs=[HERE],
        out_specs=(HERE,) * 3,
        scratch_shapes=[
            pltpu.VMEM((K * N, 3 * N), BF16),
            pltpu.VMEM((3 * N, 2 * C), BF16),
            pltpu.VMEM((8, N), F32),
        ],
        compiler_params=LIMIT,
        name="near",
    )(held(stack))


def near_kernel_stacked(stack, *refs):
    near_kernel(*(stack.at[i * ROWS : (i + 1) * ROWS] for i in range(3)), *refs)


def far_kernel(stack, total, sums_in, own_at, wide0, wide1, z_ref, w_ref, mine, theirs, s_ref, x_ref, r_ref, t_ref, part, p_ref):
    sx, sy = line(stack, SIDES), line(stack, SIDES + 1)
    right, above = sx > 0, sy > 0
    n = 0
    for i, block in ((1, wide0), (-1, wide1)):
        for j, at in ((0, 0), (1, ROWS), (-1, 2 * ROWS)):
            active = flag_of(stack, at, 1, i, j, right, above) + flag_of(block, 0, -1, i, j, right, above)
            place(block, at, line(block, at + LIVE) * active, i * sx, j * sy, p_ref, n)
            gather(block, at, x_ref, n)
            n += 1

    def store_sums(at, sums):
        for k in range(K):
            both = jnp.sum(sums[k] + sums_in[pl.ds(k * N + at, 16), :], axis=1, keepdims=True)
            r_ref[pl.ds(k * N + at, 16), :] = jnp.broadcast_to(both, (16, N))

    build(6, own_at, p_ref, s_ref, store_sums, False)
    t_ref[...] = jnp.dot(s_ref[...], x_ref[...], preferred_element_type=F32) + total[...]
    f = stack[0:N, :].astype(F32)
    g = stack[N:GEO, :].astype(F32)
    for k in range(K):
        r = r_ref[k * N : (k + 1) * N, :]
        z_ref[:, k * C : (k + 1) * C] = (r * f + t_ref[k * N : (k + 1) * N, 0:C]).astype(BF16)
        w_ref[:, k * C : (k + 1) * C] = (r * g - t_ref[k * N : (k + 1) * N, C : 2 * C]).astype(BF16)
    own_g = stack[N:GEO, :]
    part[...] = lax.dot_general(z_ref[...], own_g, (((0,), (0,)), ((), ())), preferred_element_type=F32).astype(BF16)
    core = lax.axis_index("core")
    mine[...] = part[pl.ds(pl.multiple_of(core * HALF, HALF), HALF), :]
    theirs[...] = part[pl.ds(pl.multiple_of((1 - core) * HALF, HALF), HALF), :]


def join_kernel(mine, given, out):
    at = pl.multiple_of((1 - lax.axis_index("core")) * HALF, HALF)
    out[...] = (mine[...].astype(F32) + given[pl.ds(at, HALF), :].astype(F32)).astype(BF16)


def join(mine, given):
    return pl.pallas_call(
        join_kernel,
        out_shape=pltpu.VMEM((HALF, C), BF16),
        in_specs=[HERE] * 2,
        out_specs=HERE,
        compiler_params=LIMIT,
        name="join",
    )(held(mine), held(given))


def result_kernel(z_ref, w_ref, kernels, corrected, grad):
    force = jnp.dot(z_ref[...], kernels[...], preferred_element_type=F32)
    corrected[...] = (force * KERNEL_SCALE).astype(BF16)
    back = None
    for k in range(K):
        term = lax.dot_general(
            w_ref[:, k * C : (k + 1) * C],
            kernels[k * C : (k + 1) * C, :],
            (((1,), (1,)), ((), ())),
            preferred_element_type=F32,
        )
        back = term if back is None else back + term
    grad[...] = back * KERNEL_SCALE


def results(z, w, kernels):
    return pl.pallas_call(
        result_kernel,
        out_shape=(jax.ShapeDtypeStruct((N, C), BF16), jax.ShapeDtypeStruct((N, C), F32)),
        in_specs=[HERE] * 3,
        out_specs=(HERE,) * 2,
        compiler_params=LIMIT,
        name="results",
    )(*(held(value) for value in (z, w, kernels)))


def far(stack, total, sums, own_at, wide0, wide1):
    return pl.pallas_call(
        far_kernel,
        out_shape=(
            pltpu.VMEM((N, K * C), BF16),
            pltpu.VMEM((N, K * C), BF16),
            pltpu.VMEM((HALF, C), BF16),
            pltpu.VMEM((HALF, C), BF16),
        ),
        in_specs=[HERE] * 6,
        out_specs=(HERE,) * 4,
        scratch_shapes=[
            pltpu.VMEM((K * N, 6 * N), BF16),
            pltpu.VMEM((6 * N, 2 * C), BF16),
            pltpu.VMEM((K * N, N), F32),
            pltpu.VMEM((K * N, 2 * C), F32),
            pltpu.VMEM((K * C, C), BF16),
            pltpu.VMEM((16, N), F32),
        ],
        compiler_params=LIMIT,
        name="far",
    )(*(held(value) for value in (stack, total, sums, own_at, wide0, wide1)))


def swapped(value, axes, second):
    count = lax.axis_size(axes)
    pairs = [(i, (i + 1 if (i + second) % 2 == 0 else i - 1) % count) for i in range(count)]
    return lax.ppermute(value, axes, pairs)


def exchanged(blocks, axes):
    return lax.all_to_all(blocks, axes, 0, 0, tiled=False)


def spread_kernel(blocks, out):
    total = jnp.sum(blocks[...].astype(F32), axis=0).astype(BF16)
    for i in range(out.shape[0]):
        out[i] = total


def spread(blocks, copies):
    return pl.pallas_call(
        spread_kernel,
        out_shape=pltpu.VMEM((copies,) + blocks.shape[1:], BF16),
        in_specs=[HERE],
        out_specs=HERE,
        compiler_params=LIMIT,
        name="spread",
    )(held(blocks))


def whole_sum(part):
    group, depth = lax.axis_size(GROUP), lax.axis_size(DEPTH)
    pieces = exchanged(part.reshape(group, -1, C), GROUP)
    pieces = exchanged(spread(pieces, depth), DEPTH)
    return exchanged(spread(pieces, group), GROUP).reshape(-1, C)


def body(features, offsets, counts, owned_pairs, kernels, cotangent):
    own = pack(counts, owned_pairs[0], features[0, 0], cotangent[0, 0], offsets[0, 0])
    narrow1 = swapped(own, NARROW, 1)
    narrow0 = swapped(own, NARROW, 0)
    stack = stacked(own, narrow0, narrow1)
    wide1 = swapped(stack, WIDE, 1)
    wide0 = swapped(stack, WIDE, 0)
    sums = near(stack)
    z, w, mine, theirs = far(stack, *sums, wide0, wide1)
    given = lax.all_gather(theirs, "core", axis=0, tiled=True)
    corrected, grad = results(z, w, kernels.reshape(K * C, C))
    half = join(mine, given)
    weights = lax.all_gather(whole_sum(half), "core", axis=0, tiled=True)
    scale = KERNEL_SCALE / float(lax.axis_size(WIDE) * lax.axis_size(NARROW) * N) ** 0.5
    weights = (weights.astype(F32) * scale).reshape(K, C, C)
    return corrected[None, None], grad[None, None], weights


def solution(mesh):
    split = Mesh(mesh.devices.reshape(4, 8, 4, 2, 2), ("zl", "y", "x", "zh", "core"))
    cell = P(WIDE, NARROW)
    return jax.shard_map(
        body,
        mesh=split,
        in_specs=(cell, cell, cell, cell, P(), cell),
        out_specs=(cell, cell, P()),
        check_vma=False,
    )
```

```python
import jax
import jax.numpy as jnp
from jax import lax
from jax.experimental import pallas as pl
from jax.experimental.pallas import tpu as pltpu
from jax.sharding import Mesh, PartitionSpec as P


SLOT_SHIFTS = ((0, 1), (0, -1), (-1, 0), (1, 0), (-1, 1), (1, -1), (1, 1), (-1, -1))
SLOT = {shift: index for index, shift in enumerate(SLOT_SHIFTS)}
KERNEL_SCALE = 0.0625
FAR = 64.0
K, N, C = 8, 128, 128
GEO = N
ROWS = N + 16
HALF = K * C // 2
LIVE, FLAG, SIDES = GEO + 2, GEO + 3, GEO + 11
WIDE = ("zl", "y")
NARROW = ("x", "zh", "core")
GROUP = ("y", "x")
DEPTH = ("zl", "zh")
BF16, F32 = jnp.bfloat16, jnp.float32
HERE = pl.BlockSpec(memory_space=pltpu.VMEM)
LIMIT = pltpu.CompilerParams(vmem_limit_bytes=16 << 20)


def held(value):
    return pltpu.with_memory_space_constraint(value, pltpu.VMEM)


def pack_kernel(counts, owned_hbm, features, cotangent, offsets, out, owned, off_ref, sems):
    copies = (
        pltpu.make_async_copy(offsets, off_ref, sems.at[0]),
        pltpu.make_async_copy(features, out.at[0:N], sems.at[1]),
        pltpu.make_async_copy(cotangent, out.at[ROWS : ROWS + N], sems.at[2]),
        pltpu.make_async_copy(owned_hbm, owned, sems.at[3]),
    )
    for copy in copies:
        copy.start()
    row = lax.broadcasted_iota(jnp.int32, (16, N), 0)
    lane = lax.broadcasted_iota(jnp.int32, (16, N), 1)
    copies[0].wait()
    copies[3].wait()
    off = off_ref[...].astype(F32)
    geo = jnp.where(row == 0, off[0:1, :], jnp.where(row == 1, off[1:2, :], 0.0))
    geo = jnp.where((row == 2) & (lane < counts[0, 0]), 1.0, geo)
    for s in range(8):
        geo = jnp.where(row == 3 + s, owned[0, s].astype(F32), geo)
    geo = jnp.where(row == 11, 1.0 - 2.0 * (lax.axis_index("y") % 2).astype(F32), geo)
    geo = jnp.where(row == 12, 1.0 - 2.0 * lax.axis_index("core").astype(F32), geo)
    out[GEO:ROWS, :] = geo.astype(BF16)
    copies[1].wait()
    copies[2].wait()


def pack(counts, owned, features, cotangent, offsets):
    smem = pl.BlockSpec(memory_space=pltpu.SMEM)
    hbm = pl.BlockSpec(memory_space=pltpu.HBM)
    return pl.pallas_call(
        pack_kernel,
        out_shape=pltpu.VMEM((ROWS + N, C), BF16),
        in_specs=[smem, hbm, hbm, hbm, hbm],
        out_specs=HERE,
        scratch_shapes=[pltpu.SMEM((1, 8), jnp.int32), pltpu.VMEM((2, N), BF16), pltpu.SemaphoreType.DMA((4,))],
        compiler_params=LIMIT,
        name="pack",
    )(counts, *(pltpu.with_memory_space_constraint(value, pltpu.HBM) for value in (owned, features, cotangent, offsets)))


def stack_kernel(first, second, third, out, out_g):
    for i, block in enumerate((first, second, third)):
        out[i * ROWS : (i + 1) * ROWS, :] = block[0:ROWS, :]
        out_g[i * N : (i + 1) * N, :] = block[ROWS : ROWS + N, :]


def stacked(first, second, third):
    return pl.pallas_call(
        stack_kernel,
        out_shape=(pltpu.VMEM((3 * ROWS, C), BF16), pltpu.VMEM((3 * N, C), BF16)),
        in_specs=[HERE] * 3,
        out_specs=(HERE,) * 2,
        compiler_params=LIMIT,
        name="stack",
    )(held(first), held(second), held(third))


def build(cells, own_ref, p_ref, s_ref, store_sums, double_first):
    def rows(step, carry):
        at = pl.multiple_of(step * 16, 16)
        ax = own_ref[pl.ds(at, 16), 0:N]
        ay = own_ref[pl.ds(at, 16), N : 2 * N]
        sums = [None] * K
        for n in range(cells):
            u = p_ref[2 * n : 2 * n + 1, :] - ax
            v = p_ref[2 * n + 1 : 2 * n + 2, :] - ay
            square = u * u + v * v
            t = square * (3.0 * lax.rsqrt(jnp.maximum(square, 1e-30)))
            low = jnp.maximum(1.0 - square, 0.0)
            window = low * low
            if n == 0 and double_first:
                window = window + window
            hats = (
                jnp.maximum(1.0 - t, 0.0),
                jnp.maximum(jnp.minimum(t, 2.0 - t), 0.0),
                jnp.maximum(jnp.minimum(t - 1.0, 3.0 - t), 0.0),
                jnp.maximum(t - 2.0, 0.0),
            )
            for q in range(4):
                weight = window * hats[q]
                for k, term in ((2 * q, weight * u), (2 * q + 1, weight * v)):
                    sums[k] = term if n == 0 else sums[k] + term
                    s_ref[pl.ds(k * N + at, 16), n * N : (n + 1) * N] = term.astype(BF16)
        store_sums(at, sums)
        return carry

    lax.fori_loop(0, N // 16, rows, 0)


def line(block, row):
    return block[row : row + 1, :].astype(F32)


def flag_of(block, at, flip, towards_x, towards_y, right, above):
    def row(dx, dy):
        return line(block, at + FLAG + SLOT[(-flip * dy, flip * dx)])

    def along(dx):
        if not towards_y:
            return row(dx, 0)
        return jnp.where(above, row(dx, towards_y), row(dx, -towards_y))

    if not towards_x:
        return along(0)
    return jnp.where(right, along(towards_x), along(-towards_x))


def place(block, at, use, shift_x, shift_y, p_ref, n):
    p_ref[2 * n : 2 * n + 1, :] = jnp.where(use > 0.5, line(block, at + GEO) + shift_x, -FAR)
    p_ref[2 * n + 1 : 2 * n + 2, :] = line(block, at + GEO + 1) + shift_y


def gather(block, at, x_ref, n):
    x_ref[n * N : (n + 1) * N, :] = block[at : at + N, :]


def near_kernel(own, narrow0, narrow1, total, s_ref, sums_out, own_out, x_ref, p_ref):
    sy = line(own, SIDES + 1)
    above = sy > 0
    place(own, 0, line(own, LIVE), 0.0, 0.0, p_ref, 0)
    gather(own, 0, x_ref, 0)
    for n, side, block in ((1, 1, narrow0), (2, -1, narrow1)):
        active = flag_of(own, 0, -1, 0, side, None, above) + flag_of(block, 0, 1, 0, side, None, above)
        place(block, 0, line(block, LIVE) * active, 0.0, side * sy, p_ref, n)
        gather(block, 0, x_ref, n)

    own_x = jnp.where(line(own, LIVE) > 0.5, line(own, GEO), FAR)
    own_out[:, 0:N] = jnp.broadcast_to(own_x, (N, N)).T
    own_out[:, N : 2 * N] = jnp.broadcast_to(line(own, GEO + 1), (N, N)).T

    def store_sums(at, sums):
        for k in range(K):
            sums_out[pl.ds(k * N + at, 16), :] = sums[k]

    build(3, own_out, p_ref, s_ref, store_sums, True)
    total[...] = jnp.dot(s_ref[...], x_ref[...], preferred_element_type=F32)


def near(stack):
    return pl.pallas_call(
        near_kernel_stacked,
        out_shape=(
            pltpu.VMEM((K * N, C), F32),
            pltpu.VMEM((K * N, 3 * N), BF16),
            pltpu.VMEM((K * N, N), F32),
            pltpu.VMEM((N, 2 * N), F32),
        ),
        in_specs=[HERE],
        out_specs=(HERE,) * 4,
        scratch_shapes=[
            pltpu.VMEM((3 * N, C), BF16),
            pltpu.VMEM((8, N), F32),
        ],
        compiler_params=LIMIT,
        name="near",
    )(held(stack))


def near_kernel_stacked(stack, *refs):
    near_kernel(*(stack.at[i * ROWS : (i + 1) * ROWS] for i in range(3)), *refs)


def far_kernel(stack, total, sums_in, own_at, wide0, wide1, stack_g, z_ref, s_ref, r_ref, mine, theirs, x_ref, t_ref, part, p_ref):
    sx, sy = line(stack, SIDES), line(stack, SIDES + 1)
    right, above = sx > 0, sy > 0
    n = 0
    for i, block in ((1, wide0), (-1, wide1)):
        for j, at in ((0, 0), (1, ROWS), (-1, 2 * ROWS)):
            active = flag_of(stack, at, 1, i, j, right, above) + flag_of(block, 0, -1, i, j, right, above)
            place(block, at, line(block, at + LIVE) * active, i * sx, j * sy, p_ref, n)
            gather(block, at, x_ref, n)
            n += 1

    def store_sums(at, sums):
        for k in range(K):
            both = jnp.sum(sums[k] + sums_in[pl.ds(k * N + at, 16), :], axis=1, keepdims=True)
            r_ref[pl.ds(k * N + at, 16), :] = jnp.broadcast_to(both, (16, N))

    build(6, own_at, p_ref, s_ref, store_sums, False)
    t_ref[...] = jnp.dot(s_ref[...], x_ref[...], preferred_element_type=F32) + total[...]
    f = stack[0:N, :].astype(F32)
    for k in range(K):
        r = r_ref[k * N : (k + 1) * N, :]
        z_ref[:, k * C : (k + 1) * C] = (r * f + t_ref[k * N : (k + 1) * N, :]).astype(BF16)
    part[...] = lax.dot_general(z_ref[...], stack_g[0:N, :], (((0,), (0,)), ((), ())), preferred_element_type=F32).astype(BF16)
    core = lax.axis_index("core")
    mine[...] = part[pl.ds(pl.multiple_of(core * HALF, HALF), HALF), :]
    theirs[...] = part[pl.ds(pl.multiple_of((1 - core) * HALF, HALF), HALF), :]


def join_kernel(mine, given, out):
    at = pl.multiple_of((1 - lax.axis_index("core")) * HALF, HALF)
    out[...] = (mine[...].astype(F32) + given[pl.ds(at, HALF), :].astype(F32)).astype(BF16)


def join(mine, given):
    return pl.pallas_call(
        join_kernel,
        out_shape=pltpu.VMEM((HALF, C), BF16),
        in_specs=[HERE] * 2,
        out_specs=HERE,
        compiler_params=LIMIT,
        name="join",
    )(held(mine), held(given))


def result_kernel(z_ref, near_s, far_s, r_ref, own, wide0, wide1, kernels, corrected, grad, t_ref):
    force = jnp.dot(z_ref[...], kernels[...], preferred_element_type=F32)
    corrected[...] = (force * KERNEL_SCALE).astype(BF16)
    t_ref[...] = (
        jnp.dot(near_s[...], own[...], preferred_element_type=F32)
        + jnp.dot(far_s[:, 0 : 3 * N], wide0[...], preferred_element_type=F32)
        + jnp.dot(far_s[:, 3 * N : 6 * N], wide1[...], preferred_element_type=F32)
    )
    g = own[0:N, :].astype(F32)
    back = None
    for k in range(K):
        at = slice(k * N, (k + 1) * N)
        w = (r_ref[at, :] * g - t_ref[at, :]).astype(BF16)
        term = lax.dot_general(w, kernels[at, :], (((1,), (1,)), ((), ())), preferred_element_type=F32)
        back = term if back is None else back + term
    grad[...] = back * KERNEL_SCALE


def results(*values):
    return pl.pallas_call(
        result_kernel,
        out_shape=(jax.ShapeDtypeStruct((N, C), BF16), jax.ShapeDtypeStruct((N, C), F32)),
        in_specs=[HERE] * 8,
        out_specs=(HERE,) * 2,
        scratch_shapes=[pltpu.VMEM((K * N, C), F32)],
        compiler_params=LIMIT,
        name="results",
    )(*(held(value) for value in values))


def far(*values):
    return pl.pallas_call(
        far_kernel,
        out_shape=(
            pltpu.VMEM((N, K * C), BF16),
            pltpu.VMEM((K * N, 6 * N), BF16),
            pltpu.VMEM((K * N, N), F32),
            pltpu.VMEM((HALF, C), BF16),
            pltpu.VMEM((HALF, C), BF16),
        ),
        in_specs=[HERE] * 7,
        out_specs=(HERE,) * 5,
        scratch_shapes=[
            pltpu.VMEM((6 * N, C), BF16),
            pltpu.VMEM((K * N, C), F32),
            pltpu.VMEM((K * C, C), BF16),
            pltpu.VMEM((16, N), F32),
        ],
        compiler_params=LIMIT,
        name="far",
    )(*(held(value) for value in values))


def swapped(value, axes, second):
    count = lax.axis_size(axes)
    pairs = [(i, (i + 1 if (i + second) % 2 == 0 else i - 1) % count) for i in range(count)]
    return lax.ppermute(value, axes, pairs)


def exchanged(blocks, axes):
    return lax.all_to_all(blocks, axes, 0, 0, tiled=False)


def spread_kernel(blocks, out):
    total = jnp.sum(blocks[...].astype(F32), axis=0).astype(BF16)
    for i in range(out.shape[0]):
        out[i] = total


def spread(blocks, copies):
    return pl.pallas_call(
        spread_kernel,
        out_shape=pltpu.VMEM((copies,) + blocks.shape[1:], BF16),
        in_specs=[HERE],
        out_specs=HERE,
        compiler_params=LIMIT,
        name="spread",
    )(held(blocks))


def whole_sum(part):
    group, depth = lax.axis_size(GROUP), lax.axis_size(DEPTH)
    pieces = exchanged(part.reshape(group, -1, C), GROUP)
    pieces = spread(pieces, depth)
    pieces = exchanged(pieces, DEPTH)
    pieces = spread(pieces, group)
    return exchanged(pieces, GROUP).reshape(-1, C)


def body(features, offsets, counts, owned_pairs, kernels, cotangent):
    own = pack(counts, owned_pairs[0], features[0, 0], cotangent[0, 0], offsets[0, 0])
    narrow1 = swapped(own, NARROW, 1)
    narrow0 = swapped(own, NARROW, 0)
    stack, stack_g = stacked(own, narrow0, narrow1)
    wide1 = swapped(stack, WIDE, 1)
    wide0 = swapped(stack, WIDE, 0)
    total, near_s, sums, own_at = near(stack)
    z, far_s, r, mine, theirs = far(stack, total, sums, own_at, wide0, wide1, stack_g)
    given = lax.all_gather(theirs, "core", axis=0, tiled=True)
    weights = lax.all_gather(whole_sum(join(mine, given)), "core", axis=0, tiled=True)
    wide1_g = swapped(stack_g, WIDE, 1)
    wide0_g = swapped(stack_g, WIDE, 0)
    corrected, grad = results(z, near_s, far_s, r, stack_g, wide0_g, wide1_g, kernels.reshape(K * C, C))
    scale = KERNEL_SCALE / float(lax.axis_size(WIDE) * lax.axis_size(NARROW) * N) ** 0.5
    weights = (weights.astype(F32) * scale).reshape(K, C, C)
    return corrected[None, None], grad[None, None], weights


def solution(mesh):
    split = Mesh(mesh.devices.reshape(4, 8, 4, 2, 2), ("zl", "y", "x", "zh", "core"))
    cell = P(WIDE, NARROW)
    return jax.shard_map(
        body,
        mesh=split,
        in_specs=(cell, cell, cell, cell, P(), cell),
        out_specs=(cell, cell, P()),
        check_vma=False,
    )
```

```python
import jax
import jax.numpy as jnp
from jax import lax
from jax.experimental import pallas as pl
from jax.experimental.pallas import tpu as pltpu
from jax.sharding import Mesh, PartitionSpec as P


SLOT_SHIFTS = ((0, 1), (0, -1), (-1, 0), (1, 0), (-1, 1), (1, -1), (1, 1), (-1, -1))
SLOT = {shift: index for index, shift in enumerate(SLOT_SHIFTS)}
KERNEL_SCALE = 0.0625
FAR = 64.0
K, N, C = 8, 128, 128
GEO = N
ROWS = N + 16
HALF = K * C // 2
LIVE, FLAG, SIDES = GEO + 2, GEO + 3, GEO + 11
WIDE = ("zl", "y")
NARROW = ("x", "zh", "core")
GROUP = ("x", "y")
DEPTH = ("zl", "zh")
BF16, F32 = jnp.bfloat16, jnp.float32
HERE = pl.BlockSpec(memory_space=pltpu.VMEM)
LIMIT = pltpu.CompilerParams(vmem_limit_bytes=16 << 20)


def held(value):
    return pltpu.with_memory_space_constraint(value, pltpu.VMEM)


def pack_kernel(counts, owned_hbm, features, cotangent, offsets, out, owned, off_ref, sems):
    copies = (
        pltpu.make_async_copy(offsets, off_ref, sems.at[0]),
        pltpu.make_async_copy(features, out.at[0:N], sems.at[1]),
        pltpu.make_async_copy(cotangent, out.at[ROWS : ROWS + N], sems.at[2]),
        pltpu.make_async_copy(owned_hbm, owned, sems.at[3]),
    )
    for copy in copies:
        copy.start()
    row = lax.broadcasted_iota(jnp.int32, (16, N), 0)
    lane = lax.broadcasted_iota(jnp.int32, (16, N), 1)
    copies[0].wait()
    copies[3].wait()
    off = off_ref[...].astype(F32)
    geo = jnp.where(row == 0, off[0:1, :], jnp.where(row == 1, off[1:2, :], 0.0))
    geo = jnp.where((row == 2) & (lane < counts[0, 0]), 1.0, geo)
    for s in range(8):
        geo = jnp.where(row == 3 + s, owned[0, s].astype(F32), geo)
    geo = jnp.where(row == 11, 1.0 - 2.0 * (lax.axis_index("y") % 2).astype(F32), geo)
    geo = jnp.where(row == 12, 1.0 - 2.0 * lax.axis_index("core").astype(F32), geo)
    out[GEO:ROWS, :] = geo.astype(BF16)
    copies[1].wait()
    copies[2].wait()


def pack(counts, owned, features, cotangent, offsets):
    smem = pl.BlockSpec(memory_space=pltpu.SMEM)
    hbm = pl.BlockSpec(memory_space=pltpu.HBM)
    return pl.pallas_call(
        pack_kernel,
        out_shape=pltpu.VMEM((ROWS + N, C), BF16),
        in_specs=[smem, hbm, hbm, hbm, hbm],
        out_specs=HERE,
        scratch_shapes=[pltpu.SMEM((1, 8), jnp.int32), pltpu.VMEM((2, N), BF16), pltpu.SemaphoreType.DMA((4,))],
        compiler_params=LIMIT,
        name="pack",
    )(counts, *(pltpu.with_memory_space_constraint(value, pltpu.HBM) for value in (owned, features, cotangent, offsets)))


def stack_kernel(first, second, third, out, out_g):
    for i, block in enumerate((first, second, third)):
        out[i * ROWS : (i + 1) * ROWS, :] = block[0:ROWS, :]
        out_g[i * N : (i + 1) * N, :] = block[ROWS : ROWS + N, :]


def stacked(first, second, third):
    return pl.pallas_call(
        stack_kernel,
        out_shape=(pltpu.VMEM((3 * ROWS, C), BF16), pltpu.VMEM((3 * N, C), BF16)),
        in_specs=[HERE] * 3,
        out_specs=(HERE,) * 2,
        compiler_params=LIMIT,
        name="stack",
    )(held(first), held(second), held(third))


def build(cells, own_ref, p_ref, s_ref, double_first):
    def rows(step, carry):
        at = pl.multiple_of(step * 16, 16)
        ax = own_ref[pl.ds(at, 16), 0:N]
        ay = own_ref[pl.ds(at, 16), N : 2 * N]
        for n in range(cells):
            u = p_ref[2 * n : 2 * n + 1, :] - ax
            v = p_ref[2 * n + 1 : 2 * n + 2, :] - ay
            square = u * u + v * v
            t = square * (3.0 * lax.rsqrt(jnp.maximum(square, 1e-30)))
            low = jnp.maximum(1.0 - square, 0.0)
            window = low * low
            if n == 0 and double_first:
                window = window + window
            hats = (
                jnp.maximum(1.0 - t, 0.0),
                jnp.maximum(jnp.minimum(t, 2.0 - t), 0.0),
                jnp.maximum(jnp.minimum(t - 1.0, 3.0 - t), 0.0),
                jnp.maximum(t - 2.0, 0.0),
            )
            for q in range(4):
                weight = window * hats[q]
                for k, term in ((2 * q, weight * u), (2 * q + 1, weight * v)):
                    s_ref[pl.ds(k * N + at, 16), n * N : (n + 1) * N] = term.astype(BF16)
        return carry

    lax.fori_loop(0, N // 16, rows, 0)


def line(block, row):
    return block[row : row + 1, :].astype(F32)


def flag_of(block, at, flip, towards_x, towards_y, right, above):
    def row(dx, dy):
        return line(block, at + FLAG + SLOT[(-flip * dy, flip * dx)])

    def along(dx):
        if not towards_y:
            return row(dx, 0)
        return jnp.where(above, row(dx, towards_y), row(dx, -towards_y))

    if not towards_x:
        return along(0)
    return jnp.where(right, along(towards_x), along(-towards_x))


def place(block, at, use, shift_x, shift_y, p_ref, n):
    p_ref[2 * n : 2 * n + 1, :] = jnp.where(use > 0.5, line(block, at + GEO) + shift_x, -FAR)
    p_ref[2 * n + 1 : 2 * n + 2, :] = line(block, at + GEO + 1) + shift_y


def gather(block, at, x_ref, n):
    x_ref[n * N : (n + 1) * N, 0:C] = block[at : at + N, :]
    x_ref[n * N : (n + 1) * N, C : 2 * C] = jnp.ones((N, C), BF16)


def row_of(block, j, stack, first, x_ref, p_ref):
    sx, sy = line(stack, SIDES), line(stack, SIDES + 1)
    right, above = sx > 0, sy > 0
    for n, (i, at) in enumerate(((0, 0), (1, ROWS), (-1, 2 * ROWS)), first):
        active = flag_of(block, 0, 1, i, j, right, above) + flag_of(stack, at, -1, i, j, right, above)
        place(block, at, line(block, at + LIVE) * active, i * sx, j * sy, p_ref, n)
        gather(block, at, x_ref, n)


def near_kernel(stack, chip, total, s_ref, own_out, x_ref, p_ref, beside):
    beside[...] = chip[pl.ds(pl.multiple_of((1 - lax.axis_index("core")) * (3 * ROWS), 16), 3 * ROWS), :]
    sx = line(stack, SIDES)
    right = sx > 0
    place(stack, 0, line(stack, LIVE), 0.0, 0.0, p_ref, 0)
    gather(stack, 0, x_ref, 0)
    for n, side, at in ((1, 1, ROWS), (2, -1, 2 * ROWS)):
        active = flag_of(stack, 0, 1, side, 0, right, None) + flag_of(stack, at, -1, side, 0, right, None)
        place(stack, at, line(stack, at + LIVE) * active, side * sx, 0.0, p_ref, n)
        gather(stack, at, x_ref, n)
    row_of(beside, 1, stack, 3, x_ref, p_ref)

    own_x = jnp.where(line(stack, LIVE) > 0.5, line(stack, GEO), FAR)
    own_out[:, 0:N] = jnp.broadcast_to(own_x, (N, N)).T
    own_out[:, N : 2 * N] = jnp.broadcast_to(line(stack, GEO + 1), (N, N)).T
    build(6, own_out, p_ref, s_ref, True)
    total[...] = jnp.dot(s_ref[...], x_ref[...], preferred_element_type=F32)


def near(stack, chip):
    return pl.pallas_call(
        near_kernel,
        out_shape=(
            pltpu.VMEM((K * N, 2 * C), F32),
            pltpu.VMEM((K * N, 6 * N), BF16),
            pltpu.VMEM((N, 2 * N), F32),
        ),
        in_specs=[HERE] * 2,
        out_specs=(HERE,) * 3,
        scratch_shapes=[
            pltpu.VMEM((6 * N, 2 * C), BF16),
            pltpu.VMEM((16, N), F32),
            pltpu.VMEM((3 * ROWS, C), BF16),
        ],
        compiler_params=LIMIT,
        name="near",
    )(held(stack), held(chip))


def far_kernel(stack, total, own_at, away, own_g, t_ref, s_ref, mine, theirs, x_ref, z_ref, part, p_ref):
    core = lax.axis_index("core")
    row_of(away, -1, stack, 0, x_ref, p_ref)
    build(3, own_at, p_ref, s_ref, False)
    t_ref[...] = jnp.dot(s_ref[...], x_ref[...], preferred_element_type=F32) + total[...]
    f = stack[0:N, :].astype(F32)
    for k in range(K):
        at = slice(k * N, (k + 1) * N)
        z_ref[:, at] = (t_ref[at, C : 2 * C] * f + t_ref[at, 0:C]).astype(BF16)
    part[...] = lax.dot_general(z_ref[...], own_g[0:N, :], (((0,), (0,)), ((), ())), preferred_element_type=F32).astype(BF16)
    mine[...] = part[pl.ds(pl.multiple_of(core * HALF, HALF), HALF), :]
    theirs[...] = part[pl.ds(pl.multiple_of((1 - core) * HALF, HALF), HALF), :]


def join_kernel(mine, given, out):
    at = pl.multiple_of((1 - lax.axis_index("core")) * HALF, HALF)
    out[...] = (mine[...].astype(F32) + given[pl.ds(at, HALF), :].astype(F32)).astype(BF16)


def join(mine, given):
    return pl.pallas_call(
        join_kernel,
        out_shape=pltpu.VMEM((HALF, C), BF16),
        in_specs=[HERE] * 2,
        out_specs=HERE,
        compiler_params=LIMIT,
        name="join",
    )(held(mine), held(given))


def result_kernel(sums, near_s, far_s, stack, own, chip, away, kernels, corrected, grad, t_ref):
    beside = chip[pl.ds(pl.multiple_of((1 - lax.axis_index("core")) * (3 * N), 3 * N), 3 * N), :]
    t_ref[...] = (
        jnp.dot(near_s[:, 0 : 3 * N], own[...], preferred_element_type=F32)
        + jnp.dot(near_s[:, 3 * N : 6 * N], beside, preferred_element_type=F32)
        + jnp.dot(far_s[...], away[...], preferred_element_type=F32)
    )
    f, g = stack[0:N, :].astype(F32), own[0:N, :].astype(F32)
    force = back = 0.0
    for k in range(K):
        at = slice(k * N, (k + 1) * N)
        r, matrix = sums[at, C : 2 * C], kernels[at, :]
        z = (r * f + sums[at, 0:C]).astype(BF16)
        w = (r * g - t_ref[at, :]).astype(BF16)
        force += jnp.dot(z, matrix, preferred_element_type=F32)
        back += lax.dot_general(w, matrix, (((1,), (1,)), ((), ())), preferred_element_type=F32)
    corrected[...] = (force * KERNEL_SCALE).astype(BF16)
    grad[...] = back * KERNEL_SCALE


def results(*values):
    return pl.pallas_call(
        result_kernel,
        out_shape=(jax.ShapeDtypeStruct((N, C), BF16), jax.ShapeDtypeStruct((N, C), F32)),
        in_specs=[HERE] * 8,
        out_specs=(HERE,) * 2,
        scratch_shapes=[pltpu.VMEM((K * N, C), F32)],
        compiler_params=LIMIT,
        name="results",
    )(*(held(value) for value in values))


def far(*values):
    return pl.pallas_call(
        far_kernel,
        out_shape=(
            pltpu.VMEM((K * N, 2 * C), F32),
            pltpu.VMEM((K * N, 3 * N), BF16),
            pltpu.VMEM((HALF, C), BF16),
            pltpu.VMEM((HALF, C), BF16),
        ),
        in_specs=[HERE] * 5,
        out_specs=(HERE,) * 4,
        scratch_shapes=[
            pltpu.VMEM((3 * N, 2 * C), BF16),
            pltpu.VMEM((N, K * C), BF16),
            pltpu.VMEM((K * C, C), BF16),
            pltpu.VMEM((8, N), F32),
        ],
        compiler_params=LIMIT,
        name="far",
    )(*(held(value) for value in values))


def swapped(value, axes, second):
    count = lax.axis_size(axes)
    pairs = [(i, (i + 1 if (i + second) % 2 == 0 else i - 1) % count) for i in range(count)]
    return lax.ppermute(value, axes, pairs)


def gathered(value):
    return lax.all_gather(value, "core", axis=0, tiled=True)


def exchanged(blocks, axes):
    return lax.all_to_all(blocks, axes, 0, 0, tiled=False)


def spread_kernel(blocks, out):
    total = jnp.sum(blocks[...].astype(F32), axis=0).astype(BF16)
    for i in range(out.shape[0]):
        out[i] = total


def spread(blocks, copies):
    return pl.pallas_call(
        spread_kernel,
        out_shape=pltpu.VMEM((copies,) + blocks.shape[1:], BF16),
        in_specs=[HERE],
        out_specs=HERE,
        compiler_params=LIMIT,
        name="spread",
    )(held(blocks))


def whole_sum(part):
    group, depth = lax.axis_size(GROUP), lax.axis_size(DEPTH)
    pieces = exchanged(part.reshape(group, -1, C), GROUP)
    pieces = spread(pieces, depth)
    pieces = exchanged(pieces, DEPTH)
    pieces = spread(pieces, group)
    return exchanged(pieces, GROUP).reshape(-1, C)


def body(features, offsets, counts, owned_pairs, kernels, cotangent):
    own = pack(counts, owned_pairs[0], features[0, 0], cotangent[0, 0], offsets[0, 0])
    wide1 = swapped(own, WIDE, 1)
    wide0 = swapped(own, WIDE, 0)
    stack, stack_g = stacked(own, wide0, wide1)
    away = swapped(stack, NARROW, 1)
    chip = gathered(stack)
    total, near_s, own_at = near(stack, chip)
    sums, far_s, mine, theirs = far(stack, total, own_at, away, stack_g)
    weights = gathered(whole_sum(join(mine, gathered(theirs))))
    away_g = swapped(stack_g, NARROW, 1)
    chip_g = gathered(stack_g)
    corrected, grad = results(sums, near_s, far_s, stack, stack_g, chip_g, away_g, kernels.reshape(K * C, C))
    scale = KERNEL_SCALE / float(lax.axis_size(WIDE) * lax.axis_size(NARROW) * N) ** 0.5
    weights = (weights.astype(F32) * scale).reshape(K, C, C)
    return corrected[None, None], grad[None, None], weights


def solution(mesh):
    split = Mesh(mesh.devices.reshape(4, 8, 4, 2, 2), ("zl", "y", "x", "zh", "core"))
    cell = P(WIDE, NARROW)
    return jax.shard_map(
        body,
        mesh=split,
        in_specs=(cell, cell, cell, cell, P(), cell),
        out_specs=(cell, cell, P()),
        check_vma=False,
    )
```
